256 devices in a mesh: dp: 16 (over y, z_hi), block: 16 (over z_lo, x, core).
Axes of the slice: x: 4, y: 4, z: 8 (z_hi: 4, z_lo: 2; z = z_hi * 2 + z_lo), core: 2. Of those that a mesh axis runs over, the one named last changes fastest.
Arguments:
- layer_input: bfloat16 [128, 128, 32768], P('block', None, 'dp'), may hold values from -6 to 6
- w_first: bfloat16 [128, 128, 128], P('block'), may hold values from -0.5 to 0.5
- w_second: bfloat16 [128, 128, 128], P('block'), may hold values from -0.5 to 0.5
- cotangent: bfloat16 [128, 128, 32768], P('block', None, 'dp'), may hold values from -6 to 6
Outputs:
- grad_input: bfloat16 [128, 128, 32768], P('block', None, 'dp')
- grad_first: float32 [128, 128, 128], P('block', 'dp')
- grad_second: float32 [128, 128, 128], P('block', 'dp')
- cov_in_first: float32 [128, 128, 128], P('block', 'dp')
- cov_out_first: float32 [128, 128, 128], P('block', 'dp')
- cov_in_second: float32 [128, 128, 128], P('block', 'dp')
- cov_out_second: float32 [128, 128, 128], P('block', 'dp')
The draws below stay inside these ranges and needn't reach their ends.
All inputs are finite; a program needn't handle non-finite values.
Results may differ from the reference program's by a relative error of at most 0.0049.
Values may be sent and summed in bfloat16 or wider, within the bound.
No kernel may reach another device: no remote copies, remote signals or barrier semaphores. Data moves between devices by JAX's collectives and lax.ppermute only.
A program may use at most 128 MiB of HBM per device.

```python
import math
import jax
import jax.numpy as jnp
from jax import lax

NB = 128
BS = 128
TOKENS = 32768


def with_spikes(values, rng, source, target, blocks, factor):
    def block_of(dim):
        return (jnp.arange(values.shape[dim]) // (values.shape[dim] // blocks)).reshape((-1,) + (1,) * (values.ndim - 1 - dim))

    one_side = jax.random.permutation(rng, blocks)[block_of(target)]
    far = (block_of(target) + blocks // 2) % blocks
    return jnp.where((block_of(source) == one_side) | (block_of(source) == far), factor * values, values)


def shard_levels(own_key, extent, pieces, low, largest):
    gain = 1.0
    for axis_at, blocks in pieces:
        draws = jax.random.uniform(jax.random.fold_in(jax.random.fold_in(own_key, 6), axis_at), (blocks,), jnp.float32, low / len(pieces), largest / len(pieces))
        gain = gain * jnp.repeat(jnp.exp(draws), extent[axis_at] // blocks).reshape((-1,) + (1,) * (len(extent) - 1 - axis_at))
    return gain


def noise(stream_key, dims, deviation, most, cuts=(), dtype=jnp.bfloat16):
    result = deviation * jax.random.normal(stream_key, dims, jnp.float32)
    if cuts:
        result = result * shard_levels(stream_key, dims, cuts, -0.22, 0.18)
    return jnp.clip(result, -most, most).astype(dtype)


def heavy_noise(key, shape, deviation, bound, shards, heavy, kind=jnp.bfloat16):
    values = deviation * jax.random.normal(key, shape, jnp.float32)
    if shards:
        values = values * shard_levels(key, shape, shards, -0.22, 0.18)
    return jnp.clip(with_spikes(values, jax.random.fold_in(key, 3), *heavy), -bound, bound).astype(kind)


def setup_inputs(seed: int = 0) -> dict:
    key_of = jax.random.split(jax.random.key(seed), 5)
    layer_input = heavy_noise(key_of[0], (NB, BS, TOKENS), 1.0, 6.0, ((0, 16), (2, 16)), (2, 1, 16, 2.0))
    w_first = noise(key_of[1], (NB, BS, BS), BS ** -0.5, 0.5, ((0, 16),))
    w_second = noise(key_of[2], (NB, BS, BS), BS ** -0.5, 0.5, ((0, 16),))
    cotangent = heavy_noise(key_of[3], (NB, BS, TOKENS), 1.0, 6.0, ((0, 16), (2, 16)), (2, 1, 16, 2.0))
    return {"layer_input": layer_input, "w_first": w_first, "w_second": w_second, "cotangent": cotangent}


def reference(layer_input, w_first, w_second, cotangent):
    total = layer_input.shape[2]
    root = 1.0 / math.sqrt(total)
    scale = 1.0 / total

    def first_forward(pair):
        feats, weight = pair
        return jnp.dot(weight.T, feats, preferred_element_type=jnp.float32).astype(jnp.bfloat16)
    hidden = lax.map(first_forward, (layer_input, w_first))
    mixed = jnp.transpose(hidden, (1, 0, 2))

    def second_block(items):
        perm_rows, weight, grad_rows = items
        grad_w = jnp.dot(perm_rows, grad_rows.T, preferred_element_type=jnp.float32) * root
        cov_in = jnp.dot(perm_rows, perm_rows.T, preferred_element_type=jnp.float32) * scale
        cov_out = jnp.dot(grad_rows, grad_rows.T, preferred_element_type=jnp.float32) * scale
        grad_perm = jnp.dot(weight, grad_rows, preferred_element_type=jnp.float32).astype(jnp.bfloat16)
        return (grad_w, cov_in, cov_out, grad_perm)
    grad_second, cov_in_second, cov_out_second, grad_mixed = lax.map(second_block, (mixed, w_second, cotangent))
    grad_hidden = jnp.transpose(grad_mixed, (1, 0, 2))

    def first_block(items):
        feats, weight, grad_rows = items
        grad_w = jnp.dot(feats, grad_rows.T, preferred_element_type=jnp.float32) * root
        cov_in = jnp.dot(feats, feats.T, preferred_element_type=jnp.float32) * scale
        cov_out = jnp.dot(grad_rows, grad_rows.T, preferred_element_type=jnp.float32) * scale
        grad_feats = jnp.dot(weight, grad_rows, preferred_element_type=jnp.float32).astype(jnp.bfloat16)
        return (grad_w, cov_in, cov_out, grad_feats)
    grad_first, cov_in_first, cov_out_first, grad_input = lax.map(first_block, (layer_input, w_first, grad_hidden))
    return (grad_input, grad_first, grad_second, cov_in_first, cov_out_first, cov_in_second, cov_out_second)
```

```python
import functools
import math

import jax
import jax.numpy as jnp
from jax import lax
from jax.experimental import pallas as pl
from jax.experimental.pallas import tpu as pltpu
from jax.sharding import PartitionSpec as P

BF = jnp.bfloat16
F32 = jnp.float32
NY = 4


def grad_mixed_kernel(w_ref, c_ref, o_ref):
    r = jnp.dot(w_ref[0], c_ref[0], preferred_element_type=F32)
    n, _, rows, t = o_ref.shape
    o_ref[...] = r.reshape(n, 1, rows, t).astype(BF)


def grad_mixed_send(w_second, cotangent, n):
    nb, bs, t = cotangent.shape
    return pl.pallas_call(
        grad_mixed_kernel,
        grid=(nb,),
        in_specs=[
            pl.BlockSpec((1, bs, bs), lambda j: (j, 0, 0)),
            pl.BlockSpec((1, bs, t), lambda j: (j, 0, 0)),
        ],
        out_specs=pl.BlockSpec((n, 1, bs // n, t), lambda j: (0, j, 0, 0)),
        out_shape=jax.ShapeDtypeStruct((n, nb, bs // n, t), BF),
        cost_estimate=pl.CostEstimate(
            flops=2 * nb * bs * bs * t, bytes_accessed=4 * nb * bs * t, transcendentals=0
        ),
    )(w_second, cotangent)


def second_stats_kernel(scale, root, m_ref, c_ref, o_ref):
    n, _, rows, t = m_ref.shape
    m = m_ref[...].reshape(n * rows, t)
    c = c_ref[0]
    dims = (((1,), (1,)), ((), ()))
    cov = lax.dot_general(m, m, dims, preferred_element_type=F32) * scale
    grad = lax.dot_general(m, c, dims, preferred_element_type=F32) * root
    d = o_ref.shape[0]
    o_ref[:, 0, 0] = cov.reshape(d, -1, cov.shape[1]).astype(BF)
    o_ref[:, 1, 0] = grad.reshape(d, -1, grad.shape[1]).astype(BF)


def second_stats(mixed, cotangent, scale, root, d):
    n, nb, rows, t = mixed.shape
    bs = n * rows
    return pl.pallas_call(
        functools.partial(second_stats_kernel, scale, root),
        grid=(nb,),
        in_specs=[
            pl.BlockSpec((n, 1, rows, t), lambda j: (0, j, 0, 0)),
            pl.BlockSpec((1, bs, t), lambda j: (j, 0, 0)),
        ],
        out_specs=pl.BlockSpec((d, 2, 1, bs // d, bs), lambda j: (0, 0, j, 0, 0)),
        out_shape=jax.ShapeDtypeStruct((d, 2, nb, bs // d, bs), BF),
        cost_estimate=pl.CostEstimate(
            flops=4 * nb * bs * bs * t, bytes_accessed=4 * nb * bs * t, transcendentals=0
        ),
    )(mixed, cotangent)


def ring_shift(v, stage, s):
    d = lax.axis_size("dp")
    nh = d // NY
    perm = []
    for p in range(d):
        y, h = divmod(p, nh)
        q = ((y + s) % NY) * nh + h if stage == 0 else y * nh + (h + s) % nh
        perm.append((p, q))
    return lax.ppermute(v, "dp", perm)


def exchange_sum(parts, stage, own):
    k = parts.shape[0]
    total = lax.dynamic_index_in_dim(parts, own, 0, keepdims=False)
    for s in range(1, k):
        send = lax.dynamic_index_in_dim(parts, (own + s) % k, 0, keepdims=False).astype(BF)
        total = total + ring_shift(send, stage, s).astype(F32)
    return total


def reduce_dp(stats):
    d = lax.axis_size("dp")
    nh = d // NY
    nb, bs, _ = stats[0].shape
    me = lax.axis_index("dp")
    y, h = me // nh, me % nh
    parts = jnp.stack([s.reshape(nb, NY, nh, bs // d, bs) for s in stats])
    parts = jnp.transpose(parts, (2, 3, 0, 1, 4, 5))
    after_y = exchange_sum(parts, 0, y)
    done = exchange_sum(after_y, 1, h)
    return [done[k] for k in range(len(stats))]


def per_device(layer_input, w_first, w_second, cotangent):
    nb, bs, t = layer_input.shape
    n = lax.axis_size("block")
    d = lax.axis_size("dp")
    total = t * d
    root = 1.0 / math.sqrt(total)
    scale = 1.0 / total

    gm = grad_mixed_send(w_second, cotangent, n)
    gm = lax.all_to_all(gm, "block", split_axis=0, concat_axis=0, tiled=True)

    hidden = jnp.einsum(
        "ikt,ikj->jit", layer_input, w_first, preferred_element_type=F32
    ).astype(BF)
    mixed = lax.all_to_all(
        hidden.reshape(n, bs // n, nb, t), "block", split_axis=0, concat_axis=0, tiled=True
    )
    cov_in_first = (
        jnp.einsum("ikt,ilt->ikl", layer_input, layer_input, preferred_element_type=F32) * scale
    )
    cov_out_second = (
        jnp.einsum("jmt,jnt->jmn", cotangent, cotangent, preferred_element_type=F32) * scale
    )
    grad_hidden = jnp.transpose(gm, (2, 0, 1, 3)).reshape(nb, bs, t)
    grad_first = (
        jnp.einsum("ikt,ijt->ikj", layer_input, grad_hidden, preferred_element_type=F32) * root
    )
    cov_out_first = (
        jnp.einsum("ijt,ilt->ijl", grad_hidden, grad_hidden, preferred_element_type=F32) * scale
    )
    grad_input = jnp.einsum(
        "ikj,ijt->ikt", w_first, grad_hidden, preferred_element_type=F32
    ).astype(BF)
    cov_in_first, cov_out_second, grad_first, cov_out_first = reduce_dp(
        [cov_in_first, cov_out_second, grad_first, cov_out_first]
    )
    last = second_stats(mixed, cotangent, scale, root, d)
    last = lax.all_to_all(last, "dp", split_axis=0, concat_axis=0, tiled=True)
    last = jnp.sum(last.astype(F32), axis=0)
    return (
        grad_input,
        grad_first,
        last[1],
        cov_in_first,
        cov_out_first,
        last[0],
        cov_out_second,
    )


def solution(mesh):
    in_specs = (
        P("block", None, "dp"),
        P("block", None, None),
        P("block", None, None),
        P("block", None, "dp"),
    )
    out_specs = (
        P("block", None, "dp"),
        P("block", "dp", None),
        P("block", "dp", None),
        P("block", "dp", None),
        P("block", "dp", None),
        P("block", "dp", None),
        P("block", "dp", None),
    )
    return jax.shard_map(
        per_device, mesh=mesh, in_specs=in_specs, out_specs=out_specs, check_vma=False
    )
```

```python
import functools
import math

import jax
import jax.numpy as jnp
from jax import lax
from jax.experimental import pallas as pl
from jax.experimental.pallas import tpu as pltpu
from jax.sharding import PartitionSpec as P


BF = jnp.bfloat16
F32 = jnp.float32
VMEM = pltpu.MemorySpace.VMEM
SMEM = pltpu.MemorySpace.SMEM
NT = (((1,), (1,)), ((), ()))


def params(mib):
    return pltpu.CompilerParams(vmem_limit_bytes=mib << 20)


def cost(flops, moved):
    return pl.CostEstimate(flops=flops, bytes_accessed=moved, transcendentals=0)


def in_hbm(v):
    return pltpu.with_memory_space_constraint(v, pltpu.HBM)


def fetch(src, dst, sems, b):
    return pltpu.make_async_copy(src.at[b], dst.at[b], sems.at[b])


def mix(weights_at, n, me, wbuf):
    for k in range(n):
        wbuf[k] = weights_at(me ^ k)
    a, b, c = wbuf.shape
    return wbuf[...].reshape(a * b, c)


def send_g_kernel(me_ref, w_ref, c_hbm, *refs):
    n = w_ref.shape[1]
    outs, (cbuf, wall, wbuf, sems, wsem) = refs[:n], refs[n:]
    nb, _, rows, _ = w_ref.shape
    me = me_ref[0]
    weights = pltpu.make_async_copy(w_ref, wall, wsem)
    weights.start()
    for j in range(nb):
        fetch(c_hbm, cbuf, sems, j).start()
    weights.wait()

    def step(j, carry):
        w = mix(lambda d: wall[j, d], n, me, wbuf)
        fetch(c_hbm, cbuf, sems, j).wait()
        r = jnp.dot(w, cbuf[j], preferred_element_type=F32)
        for k in range(n):
            outs[k][j] = r[k * rows : (k + 1) * rows].astype(BF)
        return carry

    lax.fori_loop(0, nb, step, 0)


def send_g(me, w_second, cotangent, n):
    nb, bs, t = cotangent.shape
    rows = bs // n
    return pl.pallas_call(
        send_g_kernel,
        in_specs=[
            pl.BlockSpec(memory_space=SMEM),
            pl.BlockSpec(memory_space=pltpu.HBM),
            pl.BlockSpec(memory_space=pltpu.HBM),
        ],
        out_specs=[pl.BlockSpec(memory_space=VMEM)] * n,
        out_shape=[pltpu.VMEM((nb, rows, t), BF)] * n,
        scratch_shapes=[
            pltpu.VMEM((nb, bs, t), BF),
            pltpu.VMEM((nb, n, rows, bs), BF),
            pltpu.VMEM((n, rows, bs), BF),
            pltpu.SemaphoreType.DMA((nb,)),
            pltpu.SemaphoreType.DMA,
        ],
        compiler_params=params(12),
        cost_estimate=cost(2 * nb * bs * bs * t, 4 * nb * bs * t),
    )(me, in_hbm(w_second.reshape(nb, n, rows, bs)), in_hbm(cotangent))


def swap_matrix(rows):
    r = lax.broadcasted_iota(jnp.int32, (rows * rows, rows * rows), 0)
    c = lax.broadcasted_iota(jnp.int32, (rows * rows, rows * rows), 1)
    return jnp.where((r % rows) * rows + r // rows == c, 1.0, 0.0).astype(BF)


def swap(p, v):
    a, b, t = v.shape
    return jnp.dot(p, v.reshape(a * b, t), preferred_element_type=F32)


def send_h_kernel(n, me_ref, w_ref, x_hbm, *refs):
    outs, (xbuf, wbuf, wt, hid, sems) = refs[:n], refs[n:]
    nb, bs, _ = w_ref.shape
    rows = bs // n
    me = me_ref[0]
    for i in range(nb):
        fetch(x_hbm, xbuf, sems, i).start()

    def step(i, carry):
        wt[...] = w_ref[i].astype(F32).T.reshape(n, rows, bs).astype(BF)
        w = mix(lambda d: wt[d], n, me, wbuf)
        fetch(x_hbm, xbuf, sems, i).wait()
        r = jnp.dot(w, xbuf[i], preferred_element_type=F32)
        for k in range(n):
            hid[k, i] = r[k * rows : (k + 1) * rows].astype(BF)
        return carry

    lax.fori_loop(0, nb, step, 0)
    p = swap_matrix(rows)
    for k in range(n):
        s = swap(p, hid[k])
        for j in range(rows):
            outs[k][j] = s[j * nb : (j + 1) * nb].astype(BF)


def send_h(me, w_first, layer_input, n):
    nb, bs, t = layer_input.shape
    rows = bs // n
    return pl.pallas_call(
        functools.partial(send_h_kernel, n),
        in_specs=[
            pl.BlockSpec(memory_space=SMEM),
            pl.BlockSpec(memory_space=VMEM),
            pl.BlockSpec(memory_space=pltpu.HBM),
        ],
        out_specs=[pl.BlockSpec(memory_space=VMEM)] * n,
        out_shape=[pltpu.VMEM((rows, nb, t), BF)] * n,
        scratch_shapes=[
            pltpu.VMEM((nb, bs, t), BF),
            pltpu.VMEM((n, rows, bs), BF),
            pltpu.VMEM((n, rows, bs), BF),
            pltpu.VMEM((n, nb, rows, t), BF),
            pltpu.SemaphoreType.DMA((nb,)),
        ],
        compiler_params=params(16),
        cost_estimate=cost(4 * nb * bs * bs * t, 4 * nb * bs * t),
    )(me, w_first, in_hbm(layer_input))


NY = 4
ORDER = (10, 6, 14, 2, 8, 4, 12, 11, 7, 15, 3, 9, 5, 13, 1)
ISSUE = (0,) + ORDER


def put(o_refs, buf, me_ref, which, b, value):
    keep, send = o_refs
    half, nh, _, _, rows, bs = keep.shape
    buf[...] = value.reshape(2, half, nh, rows, bs)
    high = lax.div(me_ref[1], half * nh)
    keep[:, :, which, b] = buf[high]
    send[:, :, which, b] = buf[1 - high].astype(BF)


def local_stats_kernel(scale, me_ref, x_ref, c_ref, *refs):
    o_refs, buf = refs[:2], refs[2]
    b = pl.program_id(0)
    x = x_ref[0]
    c = c_ref[0]
    put(o_refs, buf, me_ref, 0, b, lax.dot_general(x, x, NT, preferred_element_type=F32) * scale)
    put(o_refs, buf, me_ref, 1, b, lax.dot_general(c, c, NT, preferred_element_type=F32) * scale)


def pieces_of(nb, bs, d):
    nh = d // NY
    shape = (NY // 2, nh, 2, nb, bs // d, bs)
    spec = pl.BlockSpec(shape, lambda b: (0, 0, 0, 0, 0, 0))
    buf = pltpu.VMEM((2, NY // 2, nh, bs // d, bs), F32)
    return [spec] * 2, [jax.ShapeDtypeStruct(shape, F32), jax.ShapeDtypeStruct(shape, BF)], buf


def local_stats(me, layer_input, cotangent, scale, d):
    nb, bs, t = layer_input.shape
    out_specs, out_shape, buf = pieces_of(nb, bs, d)
    spec = pl.BlockSpec((1, bs, t), lambda b: (b, 0, 0))
    return pl.pallas_call(
        functools.partial(local_stats_kernel, scale),
        grid=(nb,),
        in_specs=[pl.BlockSpec(memory_space=SMEM), spec, spec],
        out_specs=out_specs,
        out_shape=out_shape,
        scratch_shapes=[buf],
        compiler_params=params(8),
        cost_estimate=cost(4 * nb * bs * bs * t, 4 * nb * bs * t),
    )(me, layer_input, cotangent)


def first_kernel(scale, root, n, me_ref, w_ref, x_ref, *refs):
    got = [refs[ISSUE.index(k)] for k in range(n)]
    gi_ref, o_refs, (grad, buf) = refs[n], refs[n + 1 : n + 3], refs[n + 3 :]
    nb = got[0].shape[1]
    rows = got[0].shape[0]
    me = me_ref[0]
    i = pl.program_id(0)

    @pl.when(i == 0)
    def _():
        p = swap_matrix(rows)
        for k in range(n):
            s = swap(p, got[k][...])
            for b in range(nb):
                grad[b, me ^ k] = s[b * rows : (b + 1) * rows].astype(BF)

    g = grad[i]
    g = g.reshape(g.shape[0] * g.shape[1], g.shape[2])
    x = x_ref[0]
    gi_ref[0] = jnp.dot(w_ref[0], g, preferred_element_type=F32).astype(BF)
    put(o_refs, buf, me_ref, 0, i, lax.dot_general(x, g, NT, preferred_element_type=F32) * root)
    put(o_refs, buf, me_ref, 1, i, lax.dot_general(g, g, NT, preferred_element_type=F32) * scale)


def first_block(me, w_first, layer_input, got, scale, root, d):
    n = len(got)
    nb, bs, t = layer_input.shape
    out_specs, out_shape, buf = pieces_of(nb, bs, d)
    return pl.pallas_call(
        functools.partial(first_kernel, scale, root, n),
        grid=(nb,),
        in_specs=[
            pl.BlockSpec(memory_space=SMEM),
            pl.BlockSpec((1, bs, bs), lambda i: (i, 0, 0)),
            pl.BlockSpec((1, bs, t), lambda i: (i, 0, 0)),
        ]
        + [pl.BlockSpec(memory_space=VMEM)] * n,
        out_specs=[pl.BlockSpec((1, bs, t), lambda i: (i, 0, 0))] + out_specs,
        out_shape=[jax.ShapeDtypeStruct((nb, bs, t), BF)] + out_shape,
        scratch_shapes=[pltpu.VMEM((nb, n, bs // n, t), BF), buf],
        compiler_params=params(16),
        cost_estimate=cost(8 * nb * bs * bs * t, 6 * nb * bs * t),
    )(me, w_first, layer_input, *[got[k] for k in ISSUE])


def second_kernel(scale, root, n, me_ref, c_ref, *refs):
    got = [refs[ISSUE.index(k)] for k in range(n)]
    o_ref, mixed = refs[n:]
    me = me_ref[0]
    j = pl.program_id(0)
    for k in range(n):
        mixed[me ^ k] = got[k][j]
    m = mixed[...]
    m = m.reshape(m.shape[0] * m.shape[1], m.shape[2])
    d, _, _, rows, bs = o_ref.shape
    cov = lax.dot_general(m, m, NT, preferred_element_type=F32) * scale
    grad = lax.dot_general(m, c_ref[0], NT, preferred_element_type=F32) * root
    o_ref[:, 0, j] = cov.reshape(d, rows, bs).astype(BF)
    o_ref[:, 1, j] = grad.reshape(d, rows, bs).astype(BF)


def second_block(me, cotangent, got, scale, root, d):
    n = len(got)
    nb, bs, t = cotangent.shape
    shape = (d, 2, nb, bs // d, bs)
    return pl.pallas_call(
        functools.partial(second_kernel, scale, root, n),
        grid=(nb,),
        in_specs=[
            pl.BlockSpec(memory_space=SMEM),
            pl.BlockSpec((1, bs, t), lambda j: (j, 0, 0)),
        ]
        + [pl.BlockSpec(memory_space=VMEM)] * n,
        out_specs=pl.BlockSpec(shape, lambda j: (0, 0, 0, 0, 0)),
        out_shape=jax.ShapeDtypeStruct(shape, BF),
        scratch_shapes=[pltpu.VMEM((n, bs // n, t), BF)],
        compiler_params=params(8),
        cost_estimate=cost(4 * nb * bs * bs * t, 4 * nb * bs * t),
    )(me, cotangent, *[got[k] for k in ISSUE])


def exchange(pieces):
    n = len(pieces)
    got = list(pieces)
    for k in ORDER:
        got[k] = lax.ppermute(pieces[k], "block", [(p, p ^ k) for p in range(n)])
    return [pltpu.with_memory_space_constraint(v, pltpu.VMEM) for v in got]


def halve_kernel(bit, sets, me_ref, *refs):
    keep, send, buf = refs[2 * sets :]
    width = buf.shape[-4] // sets
    for s in range(sets):
        total = refs[2 * s][...] + refs[2 * s + 1][...].astype(F32)
        if sets == 1:
            buf[...] = total.reshape(buf.shape)
        else:
            buf[:, :, s * width : (s + 1) * width] = total
    mine = lax.rem(lax.div(me_ref[1], bit), 2)
    keep[...] = buf[mine]
    send[...] = buf[1 - mine].astype(BF)


def halve(me, bit, *sets):
    shape = list(sets[0][0].shape)
    shape[-4] *= len(sets)
    if shape[0] != 2:
        shape = [2, shape[0] // 2] + shape[1:]
    elif len(shape) == 5:
        shape = [2] + shape[1:]
    out = tuple(shape[1:])
    flat = [v for pair in sets for v in pair]
    return pl.pallas_call(
        functools.partial(halve_kernel, bit, len(sets)),
        in_specs=[pl.BlockSpec(memory_space=SMEM)] + [pl.BlockSpec(memory_space=VMEM)] * len(flat),
        out_specs=[pl.BlockSpec(memory_space=VMEM)] * 2,
        out_shape=[jax.ShapeDtypeStruct(out, F32), jax.ShapeDtypeStruct(out, BF)],
        scratch_shapes=[pltpu.VMEM(tuple(shape), F32)],
        compiler_params=params(12),
        cost_estimate=cost(2 * flat[0].size, 12 * flat[0].size),
    )(me, *flat)


def swap_dp(v, bit):
    d = lax.axis_size("dp")
    return lax.ppermute(v, "dp", [(p, p ^ bit) for p in range(d)])


def finish_kernel(v_ref, keep_ref, got_ref, *o_refs):
    total = v_ref[0].astype(F32)
    for k in range(1, v_ref.shape[0]):
        total = total + v_ref[k].astype(F32)
    for s in range(total.shape[0]):
        o_refs[s][...] = total[s]
    rest = keep_ref[...] + got_ref[...].astype(F32)
    for s in range(rest.shape[0]):
        o_refs[total.shape[0] + s][...] = rest[s]


def finish(v, keep, got):
    shape = v.shape[2:]
    outs = v.shape[1] + keep.shape[0]
    return pl.pallas_call(
        finish_kernel,
        in_specs=[pl.BlockSpec(memory_space=VMEM)] * 3,
        out_specs=[pl.BlockSpec(memory_space=VMEM)] * outs,
        out_shape=[jax.ShapeDtypeStruct(shape, F32)] * outs,
        compiler_params=params(6),
        cost_estimate=cost(2 * v.size, 6 * v.size),
    )(v, keep, got)


def per_device(layer_input, w_first, w_second, cotangent):
    _, _, t = layer_input.shape
    n = lax.axis_size("block")
    d = lax.axis_size("dp")
    total = t * d
    root = 1.0 / math.sqrt(total)
    scale = 1.0 / total
    me = jnp.stack([lax.axis_index("block"), lax.axis_index("dp")]).astype(jnp.int32)

    def after(v, *done):
        return lax.optimization_barrier((v,) + done)[0]

    def after(v, *done):
        return lax.optimization_barrier((v,) + done)[0]

    out_g = send_g(me, w_second, cotangent, n)
    got_g = exchange(out_g)
    out_h = send_h(me, w_first, after(layer_input, out_g[0]), n)
    got_h = exchange(out_h)
    local = local_stats(me, after(layer_input, out_h[0]), cotangent, scale, d)
    local_got = swap_dp(local[1], d // 2)
    x3 = after(layer_input, local[0])
    grad_input, *first = first_block(me, w_first, x3, got_g, scale, root, d)
    first_got = swap_dp(first[1], d // 2)
    keep, send = halve(me, d // 4, (local[0], local_got), (first[0], first_got))
    got = swap_dp(send, d // 4)
    keep, send = halve(me, d // 8, (keep, got))
    got = swap_dp(send, d // 8)
    second = second_block(me, cotangent, got_h, scale, root, d)
    keep, send = halve(me, d // 16, (keep, got))
    got = swap_dp(send, d // 16)
    second = lax.all_to_all(second, "dp", 0, 0, tiled=True)
    cov2, grad2, cov_in1, cov_out2, grad1, cov_out1 = finish(second, keep, got)
    return (grad_input, grad1, grad2, cov_in1, cov_out1, cov2, cov_out2)


def solution(mesh):
    in_specs = (
        P("block", None, "dp"),
        P("block", None, None),
        P("block", None, None),
        P("block", None, "dp"),
    )
    out_specs = (
        P("block", None, "dp"),
        P("block", "dp", None),
        P("block", "dp", None),
        P("block", "dp", None),
        P("block", "dp", None),
        P("block", "dp", None),
        P("block", "dp", None),
    )
    return jax.shard_map(
        per_device, mesh=mesh, in_specs=in_specs, out_specs=out_specs, check_vma=False
    )
```

```python
import functools
import math

import jax
import jax.numpy as jnp
from jax import lax
from jax.experimental import pallas as pl
from jax.experimental.pallas import tpu as pltpu
from jax.sharding import PartitionSpec as P


BF = jnp.bfloat16
F32 = jnp.float32
VMEM = pltpu.MemorySpace.VMEM
SMEM = pltpu.MemorySpace.SMEM
NT = (((1,), (1,)), ((), ()))


def params(mib):
    return pltpu.CompilerParams(vmem_limit_bytes=mib << 20)


def cost(flops, moved):
    return pl.CostEstimate(flops=flops, bytes_accessed=moved, transcendentals=0)


def in_hbm(v):
    return pltpu.with_memory_space_constraint(v, pltpu.HBM)


def fetch(src, dst, sems, b):
    return pltpu.make_async_copy(src.at[b], dst.at[b], sems.at[b])


def mix(weights_at, n, me, wbuf):
    for k in range(n):
        wbuf[k] = weights_at(me ^ k)
    a, b, c = wbuf.shape
    return wbuf[...].reshape(a * b, c)


def send_g_kernel(me_ref, w_ref, c_hbm, *refs):
    n = w_ref.shape[1]
    outs, (cbuf, wall, wbuf, sems, wsem) = refs[:n], refs[n:]
    nb, _, rows, _ = w_ref.shape
    me = me_ref[0]
    weights = pltpu.make_async_copy(w_ref, wall, wsem)
    weights.start()
    for j in range(nb):
        fetch(c_hbm, cbuf, sems, j).start()
    weights.wait()

    def step(j, carry):
        w = mix(lambda d: wall[j, d], n, me, wbuf)
        fetch(c_hbm, cbuf, sems, j).wait()
        r = jnp.dot(w, cbuf[j], preferred_element_type=F32)
        for k in range(n):
            outs[k][j] = r[k * rows : (k + 1) * rows].astype(BF)
        return carry

    lax.fori_loop(0, nb, step, 0)


def send_g(me, w_second, cotangent, n):
    nb, bs, t = cotangent.shape
    rows = bs // n
    return pl.pallas_call(
        send_g_kernel,
        in_specs=[
            pl.BlockSpec(memory_space=SMEM),
            pl.BlockSpec(memory_space=pltpu.HBM),
            pl.BlockSpec(memory_space=pltpu.HBM),
        ],
        out_specs=[pl.BlockSpec(memory_space=VMEM)] * n,
        out_shape=[pltpu.VMEM((nb, rows, t), BF)] * n,
        scratch_shapes=[
            pltpu.VMEM((nb, bs, t), BF),
            pltpu.VMEM((nb, n, rows, bs), BF),
            pltpu.VMEM((n, rows, bs), BF),
            pltpu.SemaphoreType.DMA((nb,)),
            pltpu.SemaphoreType.DMA,
        ],
        compiler_params=params(12),
        cost_estimate=cost(2 * nb * bs * bs * t, 4 * nb * bs * t),
    )(me, in_hbm(w_second.reshape(nb, n, rows, bs)), in_hbm(cotangent))


def swap_matrix(rows):
    r = lax.broadcasted_iota(jnp.int32, (rows * rows, rows * rows), 0)
    c = lax.broadcasted_iota(jnp.int32, (rows * rows, rows * rows), 1)
    return jnp.where((r % rows) * rows + r // rows == c, 1.0, 0.0).astype(BF)


def swap(p, v):
    a, b, t = v.shape
    return jnp.dot(p, v.reshape(a * b, t), preferred_element_type=F32)


def send_h_kernel(n, me_ref, w_ref, x_hbm, own_ref, other_ref, xbuf, wbuf, wt, hid, sems):
    nb, bs, _ = w_ref.shape
    rows = bs // n
    me = me_ref[0]
    for i in range(nb):
        fetch(x_hbm, xbuf, sems, i).start()

    def step(i, carry):
        wt[...] = w_ref[i].astype(F32).T.reshape(n, rows, bs).astype(BF)
        w = mix(lambda d: wt[d], n, me, wbuf)
        fetch(x_hbm, xbuf, sems, i).wait()
        r = jnp.dot(w, xbuf[i], preferred_element_type=F32)
        for k in range(n):
            hid[k, i] = r[k * rows : (k + 1) * rows].astype(BF)
        return carry

    lax.fori_loop(0, nb, step, 0)
    p = swap_matrix(rows)
    for k in range(n):
        s = swap(p, hid[k])
        o_ref = other_ref if k % 2 else own_ref
        for j in range(rows):
            o_ref[k // 2, j] = s[j * nb : (j + 1) * nb].astype(BF)


def send_h(me, w_first, layer_input, n):
    nb, bs, t = layer_input.shape
    rows = bs // n
    return pl.pallas_call(
        functools.partial(send_h_kernel, n),
        in_specs=[
            pl.BlockSpec(memory_space=SMEM),
            pl.BlockSpec(memory_space=VMEM),
            pl.BlockSpec(memory_space=pltpu.HBM),
        ],
        out_specs=[pl.BlockSpec(memory_space=VMEM)] * 2,
        out_shape=[pltpu.VMEM((n // 2, rows, nb, t), BF)] * 2,
        scratch_shapes=[
            pltpu.VMEM((nb, bs, t), BF),
            pltpu.VMEM((n, rows, bs), BF),
            pltpu.VMEM((n, rows, bs), BF),
            pltpu.VMEM((n, nb, rows, t), BF),
            pltpu.SemaphoreType.DMA((nb,)),
        ],
        compiler_params=params(16),
        cost_estimate=cost(4 * nb * bs * bs * t, 4 * nb * bs * t),
    )(me, w_first, in_hbm(layer_input))


def pack_kernel(own_ref, got_ref, *o_refs):
    chips = own_ref.shape[0]
    rows = o_refs[0].shape[1]
    for part in range(PARTS):
        for q in range(chips):
            o_ref = o_refs[part * chips + q]
            o_ref[0] = own_ref[q, part * rows : (part + 1) * rows]
            o_ref[1] = got_ref[q, part * rows : (part + 1) * rows]


def pack(own, got):
    chips, rows, nb, t = own.shape
    out = pltpu.VMEM((2, rows // PARTS, nb, t), BF)
    return pl.pallas_call(
        pack_kernel,
        in_specs=[pl.BlockSpec(memory_space=VMEM)] * 2,
        out_specs=[pl.BlockSpec(memory_space=VMEM)] * (PARTS * chips),
        out_shape=[out] * (PARTS * chips),
        compiler_params=params(4),
        cost_estimate=cost(own.size, 8 * own.size),
    )(own, got)


NY = 4
ORDER = (10, 6, 14, 2, 8, 4, 12, 11, 7, 15, 3, 9, 5, 13, 1)
ISSUE = (0,) + ORDER
CHIPS = (0, 5, 3, 7, 1, 4, 2, 6)
PARTS = 2


def put(o_refs, buf, me_ref, b, value):
    keep, send = o_refs
    half, nh, _, rows, bs = keep.shape
    buf[...] = value.reshape(2, half, nh, rows, bs)
    high = lax.div(me_ref[1], half * nh)
    keep[:, :, b] = buf[high]
    send[:, :, b] = buf[1 - high].astype(BF)


def local_stats_kernel(scale, me_ref, x_ref, c_ref, *refs):
    o_refs, buf = refs[:2], refs[2]
    b = pl.program_id(0)
    x = x_ref[0]
    c = c_ref[0]
    put(o_refs, buf, me_ref, b, lax.dot_general(x, x, NT, preferred_element_type=F32) * scale)
    put(o_refs, buf, me_ref, pl.num_programs(0) + b, lax.dot_general(c, c, NT, preferred_element_type=F32) * scale)


def pieces_of(blocks, bs, d):
    nh = d // NY
    shape = (NY // 2, nh, blocks, bs // d, bs)
    spec = pl.BlockSpec(shape, lambda b: (0, 0, 0, 0, 0))
    buf = pltpu.VMEM((2, NY // 2, nh, bs // d, bs), F32)
    return [spec] * 2, [jax.ShapeDtypeStruct(shape, F32), jax.ShapeDtypeStruct(shape, BF)], buf


def local_stats(me, layer_input, cotangent, scale, d):
    nb, bs, t = layer_input.shape
    out_specs, out_shape, buf = pieces_of(2 * nb, bs, d)
    spec = pl.BlockSpec((1, bs, t), lambda b: (b, 0, 0))
    return pl.pallas_call(
        functools.partial(local_stats_kernel, scale),
        grid=(nb,),
        in_specs=[pl.BlockSpec(memory_space=SMEM), spec, spec],
        out_specs=out_specs,
        out_shape=out_shape,
        scratch_shapes=[buf],
        compiler_params=params(8),
        cost_estimate=cost(4 * nb * bs * bs * t, 4 * nb * bs * t),
    )(me, layer_input, cotangent)


def first_kernel(scale, root, n, me_ref, w_ref, x_ref, keep_in, send_in, *refs):
    got = [refs[ISSUE.index(k)] for k in range(n)]
    gi_ref, o_refs, (grad, buf) = refs[n], refs[n + 1 : n + 3], refs[n + 3 :]
    nb = got[0].shape[1]
    rows = got[0].shape[0]
    me = me_ref[0]
    i = pl.program_id(0)

    @pl.when(i == 0)
    def _():
        keep, send = o_refs
        keep[:, :, : keep_in.shape[2]] = keep_in[...]
        send[:, :, : send_in.shape[2]] = send_in[...]
        p = swap_matrix(rows)
        for k in range(n):
            s = swap(p, got[k][...])
            for b in range(nb):
                grad[b, me ^ k] = s[b * rows : (b + 1) * rows].astype(BF)

    g = grad[i]
    g = g.reshape(g.shape[0] * g.shape[1], g.shape[2])
    x = x_ref[0]
    gi_ref[0] = jnp.dot(w_ref[0], g, preferred_element_type=F32).astype(BF)
    put(o_refs, buf, me_ref, 2 * nb + i, lax.dot_general(x, g, NT, preferred_element_type=F32) * root)
    put(o_refs, buf, me_ref, 3 * nb + i, lax.dot_general(g, g, NT, preferred_element_type=F32) * scale)


def first_block(me, w_first, layer_input, local, got, scale, root, d):
    n = len(got)
    nb, bs, t = layer_input.shape
    out_specs, out_shape, buf = pieces_of(4 * nb, bs, d)
    return pl.pallas_call(
        functools.partial(first_kernel, scale, root, n),
        grid=(nb,),
        in_specs=[
            pl.BlockSpec(memory_space=SMEM),
            pl.BlockSpec((1, bs, bs), lambda i: (i, 0, 0)),
            pl.BlockSpec((1, bs, t), lambda i: (i, 0, 0)),
        ]
        + [pl.BlockSpec(memory_space=VMEM)] * (2 + n),
        out_specs=[pl.BlockSpec((1, bs, t), lambda i: (i, 0, 0))] + out_specs,
        out_shape=[jax.ShapeDtypeStruct((nb, bs, t), BF)] + out_shape,
        scratch_shapes=[pltpu.VMEM((nb, n, bs // n, t), BF), buf],
        compiler_params=params(16),
        cost_estimate=cost(8 * nb * bs * bs * t, 6 * nb * bs * t),
    )(me, w_first, layer_input, *local, *[got[k] for k in ISSUE])


def second_kernel(scale, root, n, me_ref, c_ref, *refs):
    chips = n // 2
    got = [refs[CHIPS.index(q)] for q in range(chips)]
    *o_refs, mixed = refs[chips:]
    me = me_ref[0]
    j = pl.program_id(0)
    for k in range(n):
        mixed[me ^ k] = got[k // 2][k % 2, j]
    m = mixed[...]
    m = m.reshape(m.shape[0] * m.shape[1], m.shape[2])
    cov = lax.dot_general(m, m, NT, preferred_element_type=F32) * scale
    grad = lax.dot_general(m, c_ref[0], NT, preferred_element_type=F32) * root
    if len(o_refs) == 1:
        d, _, _, rows, bs = o_refs[0].shape
        o_refs[0][:, 0, j] = cov.reshape(d, rows, bs).astype(BF)
        o_refs[0][:, 1, j] = grad.reshape(d, rows, bs).astype(BF)
    else:
        put(o_refs[:2], o_refs[2], me_ref, j, cov)
        put(o_refs[:2], o_refs[2], me_ref, pl.num_programs(0) + j, grad)


def second_block(me, cotangent, got, part, scale, root, d):
    n = 2 * len(got)
    nb, bs, t = cotangent.shape
    count = nb // PARTS
    start = part * count
    scratch = [pltpu.VMEM((n, bs // n, t), BF)]
    if part < PARTS - 1:
        out_specs, out_shape, buf = pieces_of(2 * count, bs, d)
        scratch = [buf] + scratch
    else:
        shape = (d, 2, count, bs // d, bs)
        out_specs = [pl.BlockSpec(shape, lambda j: (0, 0, 0, 0, 0))]
        out_shape = [jax.ShapeDtypeStruct(shape, BF)]
    return pl.pallas_call(
        functools.partial(second_kernel, scale, root, n),
        grid=(count,),
        in_specs=[
            pl.BlockSpec(memory_space=SMEM),
            pl.BlockSpec((1, bs, t), lambda j: (start + j, 0, 0)),
        ]
        + [pl.BlockSpec(memory_space=VMEM)] * len(got),
        out_specs=out_specs,
        out_shape=out_shape,
        scratch_shapes=scratch,
        compiler_params=params(8),
        cost_estimate=cost(4 * count * bs * bs * t, 4 * count * bs * t),
    )(me, cotangent, *[got[q] for q in CHIPS])


def halve_kernel(bit, sets, me_ref, *refs):
    keep, send, buf = refs[2 * sets :]
    at = 0
    for s in range(sets):
        total = refs[2 * s][...] + refs[2 * s + 1][...].astype(F32)
        width = total.shape[-3]
        if sets == 1:
            buf[...] = total.reshape(buf.shape)
        else:
            buf[:, :, at : at + width] = total
        at += width
    mine = lax.rem(lax.div(me_ref[1], bit), 2)
    keep[...] = buf[mine]
    send[...] = buf[1 - mine].astype(BF)


def halve(me, bit, *sets):
    shape = list(sets[0][0].shape)
    shape[-3] = sum(pair[0].shape[-3] for pair in sets)
    if shape[0] != 2:
        shape = [2, shape[0] // 2] + shape[1:]
    out = tuple(shape[1:])
    flat = [v for pair in sets for v in pair]
    return pl.pallas_call(
        functools.partial(halve_kernel, bit, len(sets)),
        in_specs=[pl.BlockSpec(memory_space=SMEM)] + [pl.BlockSpec(memory_space=VMEM)] * len(flat),
        out_specs=[pl.BlockSpec(memory_space=VMEM)] * 2,
        out_shape=[jax.ShapeDtypeStruct(out, F32), jax.ShapeDtypeStruct(out, BF)],
        scratch_shapes=[pltpu.VMEM(tuple(shape), F32)],
        compiler_params=params(12),
        cost_estimate=cost(2 * flat[0].size, 12 * flat[0].size),
    )(me, *flat)


def swap_dp(v, bit):
    d = lax.axis_size("dp")
    return lax.ppermute(v, "dp", [(p, p ^ bit) for p in range(d)])


def finish_kernel(v_ref, keep_ref, got_ref, *o_refs):
    total = v_ref[0].astype(F32)
    for k in range(1, v_ref.shape[0]):
        total = total + v_ref[k].astype(F32)
    rest = keep_ref[...] + got_ref[...].astype(F32)
    whole, split = o_refs[:4], o_refs[4:]
    nb = whole[0].shape[0]
    for s, o_ref in enumerate(whole):
        o_ref[...] = rest[s * nb : (s + 1) * nb]
    count = total.shape[1]
    for s, o_ref in enumerate(split):
        at = len(whole) * nb + s * (nb - count)
        o_ref[: nb - count] = rest[at : at + nb - count]
        o_ref[nb - count :] = total[s]


def finish(v, keep, got, nb):
    shape = (nb,) + keep.shape[1:]
    return pl.pallas_call(
        finish_kernel,
        in_specs=[pl.BlockSpec(memory_space=VMEM)] * 3,
        out_specs=[pl.BlockSpec(memory_space=VMEM)] * 6,
        out_shape=[jax.ShapeDtypeStruct(shape, F32)] * 6,
        compiler_params=params(6),
        cost_estimate=cost(2 * v.size, 6 * v.size),
    )(v, keep, got)


def swap_block(v, k):
    n = lax.axis_size("block")
    return lax.ppermute(v, "block", [(p, p ^ k) for p in range(n)])


def exchange(pieces):
    got = [pieces[0]] + [swap_block(pieces[k], k) for k in range(1, len(pieces))]
    return [pltpu.with_memory_space_constraint(v, pltpu.VMEM) for v in got]


def exchange_chips(pieces):
    got = [pieces[0]] + [swap_block(pieces[q], 2 * q) for q in range(1, len(pieces))]
    return [pltpu.with_memory_space_constraint(v, pltpu.VMEM) for v in got]


def per_device(layer_input, w_first, w_second, cotangent):
    nb, _, t = layer_input.shape
    n = lax.axis_size("block")
    d = lax.axis_size("dp")
    total = t * d
    root = 1.0 / math.sqrt(total)
    scale = 1.0 / total
    me = jnp.stack([lax.axis_index("block"), lax.axis_index("dp")]).astype(jnp.int32)

    def after(v, *done):
        return lax.optimization_barrier((v,) + done)[0]

    def after(v, *done):
        return lax.optimization_barrier((v,) + done)[0]

    out_g = send_g(me, w_second, cotangent, n)
    got_g = exchange(out_g)
    own, other = send_h(me, w_first, after(layer_input, out_g[0]), n)
    other = swap_block(other, 1)
    local = local_stats(me, after(layer_input, own), cotangent, scale, d)
    packed = pack(own, pltpu.with_memory_space_constraint(other, pltpu.VMEM))
    got_h1 = exchange_chips(packed[: n // 2])
    got_h2 = exchange_chips(packed[n // 2 :])
    x3 = after(layer_input, packed[0])
    grad_input, *first = first_block(me, w_first, x3, local, got_g, scale, root, d)
    first_got = swap_dp(first[1], d // 2)
    c2 = after(cotangent, first[0])
    half = second_block(me, c2, got_h1, 0, scale, root, d)
    half_got = swap_dp(half[1], d // 2)
    keep, send = halve(me, d // 4, (first[0], first_got), (half[0], half_got))
    got = swap_dp(send, d // 4)
    keep, send = halve(me, d // 8, (keep, got))
    got = swap_dp(send, d // 8)
    c3 = after(cotangent, half[0])
    (second,) = second_block(me, c3, got_h2, 1, scale, root, d)
    keep, send = halve(me, d // 16, (keep, got))
    got = swap_dp(send, d // 16)
    second = lax.all_to_all(second, "dp", 0, 0, tiled=True)
    cov_in1, cov_out2, grad1, cov_out1, cov2, grad2 = finish(second, keep, got, nb)
    return (grad_input, grad1, grad2, cov_in1, cov_out1, cov2, cov_out2)


def solution(mesh):
    in_specs = (
        P("block", None, "dp"),
        P("block", None, None),
        P("block", None, None),
        P("block", None, "dp"),
    )
    out_specs = (
        P("block", None, "dp"),
        P("block", "dp", None),
        P("block", "dp", None),
        P("block", "dp", None),
        P("block", "dp", None),
        P("block", "dp", None),
        P("block", "dp", None),
    )
    return jax.shard_map(
        per_device, mesh=mesh, in_specs=in_specs, out_specs=out_specs, check_vma=False
    )
```

```python
import functools
import math

import jax
import jax.numpy as jnp
from jax import lax
from jax.experimental import pallas as pl
from jax.experimental.pallas import tpu as pltpu
from jax.sharding import PartitionSpec as P


BF = jnp.bfloat16
F32 = jnp.float32
VMEM = pltpu.MemorySpace.VMEM
SMEM = pltpu.MemorySpace.SMEM
NT = (((1,), (1,)), ((), ()))


def params(mib):
    return pltpu.CompilerParams(vmem_limit_bytes=mib << 20)


def cost(flops, moved):
    return pl.CostEstimate(flops=flops, bytes_accessed=moved, transcendentals=0)


def in_hbm(v):
    return pltpu.with_memory_space_constraint(v, pltpu.HBM)


def fetch(src, dst, sems, b):
    return pltpu.make_async_copy(src.at[b], dst.at[b], sems.at[b])


def mix(weights_at, steps, me, wbuf):
    for m, k in enumerate(steps):
        wbuf[m] = weights_at(me ^ k)
    a, b, c = wbuf.shape
    return wbuf[...].reshape(a * b, c)


def send_g_kernel(steps, me_ref, w_ref, c_hbm, *refs):
    count = len(steps)
    outs, (cbuf, wall, wbuf, sems, wsem) = refs[:count], refs[count:]
    nb, _, rows, _ = w_ref.shape
    me = me_ref[0]
    weights = pltpu.make_async_copy(w_ref, wall, wsem)
    weights.start()
    for j in range(nb):
        fetch(c_hbm, cbuf, sems, j).start()
    weights.wait()

    def step(j, carry):
        w = mix(lambda d: wall[j, d], steps, me, wbuf)
        fetch(c_hbm, cbuf, sems, j).wait()
        r = jnp.dot(w, cbuf[j], preferred_element_type=F32)
        for m in range(count):
            outs[m][j] = r[m * rows : (m + 1) * rows].astype(BF)
        return carry

    lax.fori_loop(0, nb, step, 0)


def send_g(me, w_second, cotangent, n, steps):
    nb, bs, t = cotangent.shape
    rows = bs // n
    count = len(steps)
    return pl.pallas_call(
        functools.partial(send_g_kernel, steps),
        in_specs=[
            pl.BlockSpec(memory_space=SMEM),
            pl.BlockSpec(memory_space=pltpu.HBM),
            pl.BlockSpec(memory_space=pltpu.HBM),
        ],
        out_specs=[pl.BlockSpec(memory_space=VMEM)] * count,
        out_shape=[pltpu.VMEM((nb, rows, t), BF)] * count,
        scratch_shapes=[
            pltpu.VMEM((nb, bs, t), BF),
            pltpu.VMEM((nb, n, rows, bs), BF),
            pltpu.VMEM((count, rows, bs), BF),
            pltpu.SemaphoreType.DMA((nb,)),
            pltpu.SemaphoreType.DMA,
        ],
        compiler_params=params(12),
        cost_estimate=cost(2 * nb * count * rows * bs * t, 4 * nb * bs * t),
    )(me, in_hbm(w_second.reshape(nb, n, rows, bs)), in_hbm(cotangent))


def swap_matrix(rows):
    r = lax.broadcasted_iota(jnp.int32, (rows * rows, rows * rows), 0)
    c = lax.broadcasted_iota(jnp.int32, (rows * rows, rows * rows), 1)
    return jnp.where((r % rows) * rows + r // rows == c, 1.0, 0.0).astype(BF)


def swap(p, v):
    a, b, t = v.shape
    return jnp.dot(p, v.reshape(a * b, t), preferred_element_type=F32)


def send_h_kernel(n, me_ref, w_ref, x_hbm, own_ref, other_ref, xbuf, wbuf, wt, hid, sems):
    nb, bs, _ = w_ref.shape
    rows = bs // n
    me = me_ref[0]
    for i in range(nb):
        fetch(x_hbm, xbuf, sems, i).start()

    def step(i, carry):
        wt[...] = w_ref[i].astype(F32).T.reshape(n, rows, bs).astype(BF)
        w = mix(lambda d: wt[d], range(n), me, wbuf)
        fetch(x_hbm, xbuf, sems, i).wait()
        r = jnp.dot(w, xbuf[i], preferred_element_type=F32)
        for k in range(n):
            hid[k, i] = r[k * rows : (k + 1) * rows].astype(BF)
        return carry

    lax.fori_loop(0, nb, step, 0)
    p = swap_matrix(rows)
    for k in range(n):
        s = swap(p, hid[k])
        o_ref = other_ref if k % 2 else own_ref
        for j in range(rows):
            o_ref[k // 2, j] = s[j * nb : (j + 1) * nb].astype(BF)


def send_h(me, w_first, layer_input, n):
    nb, bs, t = layer_input.shape
    rows = bs // n
    return pl.pallas_call(
        functools.partial(send_h_kernel, n),
        in_specs=[
            pl.BlockSpec(memory_space=SMEM),
            pl.BlockSpec(memory_space=VMEM),
            pl.BlockSpec(memory_space=pltpu.HBM),
        ],
        out_specs=[pl.BlockSpec(memory_space=VMEM)] * 2,
        out_shape=[pltpu.VMEM((n // 2, rows, nb, t), BF)] * 2,
        scratch_shapes=[
            pltpu.VMEM((nb, bs, t), BF),
            pltpu.VMEM((n, rows, bs), BF),
            pltpu.VMEM((n, rows, bs), BF),
            pltpu.VMEM((n, nb, rows, t), BF),
            pltpu.SemaphoreType.DMA((nb,)),
        ],
        compiler_params=params(16),
        cost_estimate=cost(4 * nb * bs * bs * t, 4 * nb * bs * t),
    )(me, w_first, in_hbm(layer_input))


def pack_kernel(own_ref, got_ref, *o_refs):
    chips = own_ref.shape[0]
    rows = o_refs[0].shape[1]
    for part in range(PARTS):
        for q in range(chips):
            o_ref = o_refs[part * chips + q]
            o_ref[0] = own_ref[q, part * rows : (part + 1) * rows]
            o_ref[1] = got_ref[q, part * rows : (part + 1) * rows]


def pack(own, got):
    chips, rows, nb, t = own.shape
    out = pltpu.VMEM((2, rows // PARTS, nb, t), BF)
    return pl.pallas_call(
        pack_kernel,
        in_specs=[pl.BlockSpec(memory_space=VMEM)] * 2,
        out_specs=[pl.BlockSpec(memory_space=VMEM)] * (PARTS * chips),
        out_shape=[out] * (PARTS * chips),
        compiler_params=params(4),
        cost_estimate=cost(own.size, 8 * own.size),
    )(own, got)


NY = 4
ORDER = (12, 10, 6, 14, 2, 8, 4, 1, 11, 7, 15, 3, 9, 5, 13)
ISSUE = (0,) + ORDER
SOON, LATER = ORDER[:7], ORDER[7:] + (0,)
CHIPS = (0, 5, 3, 7, 1, 4, 2, 6)
PARTS = 2


def put(o_refs, buf, me_ref, b, value):
    keep, send = o_refs
    half, nh, _, rows, bs = keep.shape
    buf[...] = value.reshape(2, half, nh, rows, bs)
    high = lax.div(me_ref[1], half * nh)
    keep[:, :, b] = buf[high]
    send[:, :, b] = buf[1 - high].astype(BF)


def local_stats_kernel(scale, me_ref, x_ref, c_ref, *refs):
    o_refs, buf = refs[:2], refs[2]
    b = pl.program_id(0)
    x = x_ref[0]
    c = c_ref[0]
    put(o_refs, buf, me_ref, b, lax.dot_general(x, x, NT, preferred_element_type=F32) * scale)
    put(o_refs, buf, me_ref, pl.num_programs(0) + b, lax.dot_general(c, c, NT, preferred_element_type=F32) * scale)


def pieces_of(blocks, bs, d):
    nh = d // NY
    shape = (NY // 2, nh, blocks, bs // d, bs)
    spec = pl.BlockSpec(shape, lambda b: (0, 0, 0, 0, 0))
    buf = pltpu.VMEM((2, NY // 2, nh, bs // d, bs), F32)
    return [spec] * 2, [jax.ShapeDtypeStruct(shape, F32), jax.ShapeDtypeStruct(shape, BF)], buf


def local_stats(me, layer_input, cotangent, scale, d):
    nb, bs, t = layer_input.shape
    out_specs, out_shape, buf = pieces_of(2 * nb, bs, d)
    spec = pl.BlockSpec((1, bs, t), lambda b: (b, 0, 0))
    return pl.pallas_call(
        functools.partial(local_stats_kernel, scale),
        grid=(nb,),
        in_specs=[pl.BlockSpec(memory_space=SMEM), spec, spec],
        out_specs=out_specs,
        out_shape=out_shape,
        scratch_shapes=[buf],
        compiler_params=params(8),
        cost_estimate=cost(4 * nb * bs * bs * t, 4 * nb * bs * t),
    )(me, layer_input, cotangent)


def first_kernel(scale, root, n, me_ref, w_ref, x_ref, keep_in, send_in, *refs):
    got = [refs[ISSUE.index(k)] for k in range(n)]
    gi_ref, o_refs, (grad, buf) = refs[n], refs[n + 1 : n + 3], refs[n + 3 :]
    nb = got[0].shape[1]
    rows = got[0].shape[0]
    me = me_ref[0]
    i = pl.program_id(0)

    @pl.when(i == 0)
    def _():
        keep, send = o_refs
        keep[:, :, : keep_in.shape[2]] = keep_in[...]
        send[:, :, : send_in.shape[2]] = send_in[...]
        p = swap_matrix(rows)
        for k in range(n):
            s = swap(p, got[k][...])
            for b in range(nb):
                grad[b, me ^ k] = s[b * rows : (b + 1) * rows].astype(BF)

    g = grad[i]
    g = g.reshape(g.shape[0] * g.shape[1], g.shape[2])
    x = x_ref[0]
    gi_ref[0] = jnp.dot(w_ref[0], g, preferred_element_type=F32).astype(BF)
    put(o_refs, buf, me_ref, 2 * nb + i, lax.dot_general(x, g, NT, preferred_element_type=F32) * root)
    put(o_refs, buf, me_ref, 3 * nb + i, lax.dot_general(g, g, NT, preferred_element_type=F32) * scale)


def first_block(me, w_first, layer_input, local, got, scale, root, d):
    n = len(got)
    nb, bs, t = layer_input.shape
    out_specs, out_shape, buf = pieces_of(4 * nb, bs, d)
    return pl.pallas_call(
        functools.partial(first_kernel, scale, root, n),
        grid=(nb,),
        in_specs=[
            pl.BlockSpec(memory_space=SMEM),
            pl.BlockSpec((1, bs, bs), lambda i: (i, 0, 0)),
            pl.BlockSpec((1, bs, t), lambda i: (i, 0, 0)),
        ]
        + [pl.BlockSpec(memory_space=VMEM)] * (2 + n),
        out_specs=[pl.BlockSpec((1, bs, t), lambda i: (i, 0, 0))] + out_specs,
        out_shape=[jax.ShapeDtypeStruct((nb, bs, t), BF)] + out_shape,
        scratch_shapes=[pltpu.VMEM((nb, n, bs // n, t), BF), buf],
        compiler_params=params(16),
        cost_estimate=cost(8 * nb * bs * bs * t, 6 * nb * bs * t),
    )(me, w_first, layer_input, *local, *[got[k] for k in ISSUE])


def second_kernel(scale, root, n, me_ref, c_ref, *refs):
    chips = n // 2
    got = [refs[CHIPS.index(q)] for q in range(chips)]
    *o_refs, mixed = refs[chips:]
    me = me_ref[0]
    j = pl.program_id(0)
    for k in range(n):
        mixed[me ^ k] = got[k // 2][k % 2, j]
    m = mixed[...]
    m = m.reshape(m.shape[0] * m.shape[1], m.shape[2])
    cov = lax.dot_general(m, m, NT, preferred_element_type=F32) * scale
    grad = lax.dot_general(m, c_ref[0], NT, preferred_element_type=F32) * root
    if len(o_refs) == 1:
        d, _, _, rows, bs = o_refs[0].shape
        o_refs[0][:, 0, j] = cov.reshape(d, rows, bs).astype(BF)
        o_refs[0][:, 1, j] = grad.reshape(d, rows, bs).astype(BF)
    else:
        put(o_refs[:2], o_refs[2], me_ref, j, cov)
        put(o_refs[:2], o_refs[2], me_ref, pl.num_programs(0) + j, grad)


def second_block(me, cotangent, got, part, scale, root, d):
    n = 2 * len(got)
    nb, bs, t = cotangent.shape
    count = nb // PARTS
    start = part * count
    scratch = [pltpu.VMEM((n, bs // n, t), BF)]
    if part < PARTS - 1:
        out_specs, out_shape, buf = pieces_of(2 * count, bs, d)
        scratch = [buf] + scratch
    else:
        shape = (d, 2, count, bs // d, bs)
        out_specs = [pl.BlockSpec(shape, lambda j: (0, 0, 0, 0, 0))]
        out_shape = [jax.ShapeDtypeStruct(shape, BF)]
    return pl.pallas_call(
        functools.partial(second_kernel, scale, root, n),
        grid=(count,),
        in_specs=[
            pl.BlockSpec(memory_space=SMEM),
            pl.BlockSpec((1, bs, t), lambda j: (start + j, 0, 0)),
        ]
        + [pl.BlockSpec(memory_space=VMEM)] * len(got),
        out_specs=out_specs,
        out_shape=out_shape,
        scratch_shapes=scratch,
        compiler_params=params(8),
        cost_estimate=cost(4 * count * bs * bs * t, 4 * count * bs * t),
    )(me, cotangent, *[got[q] for q in CHIPS])


def halve_kernel(bit, sets, me_ref, *refs):
    keep, send, buf = refs[2 * sets :]
    at = 0
    for s in range(sets):
        total = refs[2 * s][...] + refs[2 * s + 1][...].astype(F32)
        width = total.shape[-3]
        if sets == 1:
            buf[...] = total.reshape(buf.shape)
        else:
            buf[:, :, at : at + width] = total
        at += width
    mine = lax.rem(lax.div(me_ref[1], bit), 2)
    keep[...] = buf[mine]
    send[...] = buf[1 - mine].astype(BF)


def halve(me, bit, *sets):
    shape = list(sets[0][0].shape)
    shape[-3] = sum(pair[0].shape[-3] for pair in sets)
    if shape[0] != 2:
        shape = [2, shape[0] // 2] + shape[1:]
    out = tuple(shape[1:])
    flat = [v for pair in sets for v in pair]
    return pl.pallas_call(
        functools.partial(halve_kernel, bit, len(sets)),
        in_specs=[pl.BlockSpec(memory_space=SMEM)] + [pl.BlockSpec(memory_space=VMEM)] * len(flat),
        out_specs=[pl.BlockSpec(memory_space=VMEM)] * 2,
        out_shape=[jax.ShapeDtypeStruct(out, F32), jax.ShapeDtypeStruct(out, BF)],
        scratch_shapes=[pltpu.VMEM(tuple(shape), F32)],
        compiler_params=params(12),
        cost_estimate=cost(2 * flat[0].size, 12 * flat[0].size),
    )(me, *flat)


def swap_dp(v, bit):
    d = lax.axis_size("dp")
    return lax.ppermute(v, "dp", [(p, p ^ bit) for p in range(d)])


def finish_kernel(v_ref, keep_ref, got_ref, *o_refs):
    total = v_ref[0].astype(F32)
    for k in range(1, v_ref.shape[0]):
        total = total + v_ref[k].astype(F32)
    rest = keep_ref[...] + got_ref[...].astype(F32)
    whole, split = o_refs[:4], o_refs[4:]
    nb = whole[0].shape[0]
    for s, o_ref in enumerate(whole):
        o_ref[...] = rest[s * nb : (s + 1) * nb]
    count = total.shape[1]
    for s, o_ref in enumerate(split):
        at = len(whole) * nb + s * (nb - count)
        o_ref[: nb - count] = rest[at : at + nb - count]
        o_ref[nb - count :] = total[s]


def finish(v, keep, got, nb):
    shape = (nb,) + keep.shape[1:]
    return pl.pallas_call(
        finish_kernel,
        in_specs=[pl.BlockSpec(memory_space=VMEM)] * 3,
        out_specs=[pl.BlockSpec(memory_space=VMEM)] * 6,
        out_shape=[jax.ShapeDtypeStruct(shape, F32)] * 6,
        compiler_params=params(6),
        cost_estimate=cost(2 * v.size, 6 * v.size),
    )(v, keep, got)


def swap_block(v, k):
    n = lax.axis_size("block")
    return lax.ppermute(v, "block", [(p, p ^ k) for p in range(n)])


def exchange(steps, pieces):
    got = {k: v if k == 0 else swap_block(v, k) for k, v in zip(steps, pieces)}
    return {k: pltpu.with_memory_space_constraint(v, pltpu.VMEM) for k, v in got.items()}


def exchange_chips(pieces):
    got = [pieces[0]] + [swap_block(pieces[q], 2 * q) for q in range(1, len(pieces))]
    return [pltpu.with_memory_space_constraint(v, pltpu.VMEM) for v in got]


def per_device(layer_input, w_first, w_second, cotangent):
    nb, _, t = layer_input.shape
    n = lax.axis_size("block")
    d = lax.axis_size("dp")
    total = t * d
    root = 1.0 / math.sqrt(total)
    scale = 1.0 / total
    me = jnp.stack([lax.axis_index("block"), lax.axis_index("dp")]).astype(jnp.int32)

    def after(v, *done):
        return lax.optimization_barrier((v,) + done)[0]

    def after(v, *done):
        return lax.optimization_barrier((v,) + done)[0]

    out_g1 = send_g(me, w_second, cotangent, n, SOON)
    got_g1 = exchange(SOON, out_g1)
    out_g2 = send_g(me, w_second, after(cotangent, out_g1[0]), n, LATER)
    got_g2 = exchange(LATER, out_g2)
    got_g = [(got_g1 | got_g2)[k] for k in range(n)]
    own, other = send_h(me, w_first, after(layer_input, out_g2[0]), n)
    other = swap_block(other, 1)
    local = local_stats(me, after(layer_input, own), cotangent, scale, d)
    packed = pack(own, pltpu.with_memory_space_constraint(other, pltpu.VMEM))
    got_h1 = exchange_chips(packed[: n // 2])
    got_h2 = exchange_chips(packed[n // 2 :])
    x3 = after(layer_input, packed[0])
    grad_input, *first = first_block(me, w_first, x3, local, got_g, scale, root, d)
    first_got = swap_dp(first[1], d // 2)
    c2 = after(cotangent, first[0])
    half = second_block(me, c2, got_h1, 0, scale, root, d)
    half_got = swap_dp(half[1], d // 2)
    keep, send = halve(me, d // 4, (first[0], first_got), (half[0], half_got))
    got = swap_dp(send, d // 4)
    keep, send = halve(me, d // 8, (keep, got))
    got = swap_dp(send, d // 8)
    c3 = after(cotangent, half[0])
    (second,) = second_block(me, c3, got_h2, 1, scale, root, d)
    keep, send = halve(me, d // 16, (keep, got))
    got = swap_dp(send, d // 16)
    second = lax.all_to_all(second, "dp", 0, 0, tiled=True)
    cov_in1, cov_out2, grad1, cov_out1, cov2, grad2 = finish(second, keep, got, nb)
    return (grad_input, grad1, grad2, cov_in1, cov_out1, cov2, cov_out2)


def solution(mesh):
    in_specs = (
        P("block", None, "dp"),
        P("block", None, None),
        P("block", None, None),
        P("block", None, "dp"),
    )
    out_specs = (
        P("block", None, "dp"),
        P("block", "dp", None),
        P("block", "dp", None),
        P("block", "dp", None),
        P("block", "dp", None),
        P("block", "dp", None),
        P("block", "dp", None),
    )
    return jax.shard_map(
        per_device, mesh=mesh, in_specs=in_specs, out_specs=out_specs, check_vma=False
    )
```
